256 devices in a mesh: tx: 16 (over z, core), ty: 16 (over y, x).
Axes of the slice: x: 4, y: 4, z: 8, core: 2. Of those that a mesh axis runs over, the one named last changes fastest.
Arguments:
- skeleton: float32 [1, 8192, 8192], P(None, 'tx', 'ty'), as said below
- generator: float32 [1, 8192, 8192], P(None, 'tx', 'ty'), may hold values from -0.1875 to 0.1875
- skeleton_lists: int32 [1, 16, 8192], P(None, 'ty', 'tx'), may hold values from 0 to 1023, as said below
- upper_lists: int32 [1, 16, 4096], P(None, 'ty', 'tx'), may hold values from 0 to 1023, as said below
Outputs:
- factor_low: float32 [1, 8192, 4096], P(None, 'tx', 'ty')
- panel_low: float32 [1, 8192, 4096], P(None, 'tx', 'ty')
- factor_high: float32 [1, 8192, 2048], P(None, 'tx', 'ty')
- panel_high: float32 [1, 8192, 2048], P(None, 'tx', 'ty')
- schur_high: float32 [1, 8192, 2048], P(None, 'tx', 'ty')
The draws below stay inside these ranges and needn't reach their ends.
Inputs may be any that keep to these rules, and one draw needn't show every extreme that they name: `skeleton_lists`: the 1024 entries of each merged node's list are a permutation of 0 to 1023. `upper_lists`: the four quarters of each second level node's list together are a permutation of 0 to 1023. `skeleton`: each 512 x 512 block is symmetric, and its smallest eigenvalue is 5 or more.
All inputs are finite; a program needn't handle non-finite values.
Results may differ from the reference program's by a relative error of at most 0.000075.
Values sent between devices are 32-bit elements; how exact they have to be, the bound alone decides.
No kernel may reach another device: no remote copies, remote signals or barrier semaphores. Data moves between devices by JAX's collectives and lax.ppermute only.
A program may use at most 64 MiB of HBM per device.

```python
import jax
import jax.numpy as jnp
from jax import lax

R = 512
BANDS = 1
NODE_X = 8
NODE_Y = 8
N_TX = 16
N_TY = 16


def draw_skeleton(key, part):
    first_key, second_key = jax.random.split(jax.random.fold_in(key, 11))
    block_shape = (BANDS, 2 * NODE_X, 2 * NODE_Y, R, R)
    factors = jax.random.normal(first_key, block_shape, jnp.float32)
    diagonal = jax.random.uniform(second_key, block_shape[:-1], jnp.float32, 5.0, 8.0)
    dense = jnp.einsum('abcik,abcjk->abcij', factors, factors, precision=lax.Precision.HIGHEST, preferred_element_type=jnp.float32) * (4.0 / R)
    dense = 0.5 * (dense + jnp.swapaxes(dense, -1, -2))
    identity = jnp.eye(R, dtype=jnp.float32)
    blocks = dense + identity * diagonal[..., :, None]
    return blocks.transpose(0, 1, 3, 2, 4).reshape(BANDS, 2 * NODE_X * R, 2 * NODE_Y * R)


def node_perms(key, count):
    keys = jax.random.split(key, count)
    return jax.vmap(lambda single: jax.random.permutation(single, 2 * R))(keys).astype(jnp.int32)


def draw_skeleton_lists(key, part):
    perms = node_perms(jax.random.fold_in(key, 23), BANDS * 2 * NODE_Y * NODE_X)
    shaped = perms.reshape(BANDS, 2 * NODE_Y, NODE_X, 2, R).transpose(0, 1, 3, 2, 4)
    return shaped.reshape(BANDS, 2 * NODE_Y, NODE_X * 2 * R)


def draw_upper_lists(key, part):
    perms = node_perms(jax.random.fold_in(key, 37), BANDS * NODE_X * NODE_Y)
    shaped = perms.reshape(BANDS, NODE_X, NODE_Y, 2, 2, R // 2).transpose(0, 3, 2, 4, 1, 5)
    return shaped.reshape(BANDS, 2 * NODE_Y, NODE_X * R)


def block_levels(rng, dims, cuts, smallest, largest):
    level, own = 1.0, jax.random.fold_in(rng, 6)
    for position, shards_of in cuts:
        steps = jnp.exp(jax.random.uniform(jax.random.fold_in(own, position), (shards_of,), jnp.float32, smallest / len(cuts), largest / len(cuts)))
        level = level * jnp.repeat(steps, dims[position] // shards_of).reshape([-1 if axis == position else 1 for axis in range(len(dims))])
    return level


def centred(own_key, dims, width, limit, cuts=(), held_as=jnp.bfloat16):
    level = block_levels(own_key, dims, cuts, -0.22, 0.18) if cuts else 1.0
    drawn = jax.random.normal(own_key, dims, jnp.float32) * width * level
    return jnp.minimum(jnp.maximum(drawn, -limit), limit).astype(held_as)


def setup_inputs(seed: int = 0) -> dict:
    key_of = jax.random.split(jax.random.key(seed), 5)
    skeleton = draw_skeleton(jax.random.fold_in(key_of[4], 71), 0)
    generator = centred(key_of[1], (BANDS, N_TX * R, N_TY * R), (2 * R) ** -0.5, 0.1875, ((1, 16), (2, 16)), jnp.float32)
    skeleton_lists = draw_skeleton_lists(jax.random.fold_in(key_of[4], 71), 0)
    upper_lists = draw_upper_lists(jax.random.fold_in(key_of[4], 71), 0)
    return dict(skeleton=skeleton, generator=generator, skeleton_lists=skeleton_lists, upper_lists=upper_lists)


def merge_one(upper_block, lower_block, gen_first, gen_second, order_one):
    width_all = upper_block.shape[0]
    coupling = jnp.dot(gen_first.astype(jnp.float32), gen_second.T.astype(jnp.float32), precision=lax.Precision.HIGHEST, preferred_element_type=jnp.float32)
    merged = jnp.concatenate((jnp.concatenate((upper_block, coupling), 1), jnp.concatenate((coupling.T, lower_block), 1)), 0)
    arranged = jnp.take(jnp.take(merged, order_one, axis=0), order_one, axis=1)
    factor = jnp.linalg.cholesky(arranged[:width_all, :width_all])
    panel_all = jax.scipy.linalg.solve_triangular(factor, arranged[:width_all, width_all:], lower=True)
    schur_all = arranged[width_all:, width_all:] - jnp.dot(panel_all.T.astype(jnp.float32), panel_all.astype(jnp.float32), precision=lax.Precision.HIGHEST, preferred_element_type=jnp.float32)
    stacked = jnp.concatenate((gen_first, gen_second), 0)
    gen_parent = jnp.take(stacked, order_one[width_all:], axis=0)
    return (factor, panel_all, schur_all, gen_parent)

def flatten_nodes(array_in):
    return array_in.reshape((-1,) + array_in.shape[3:])

def run_level(inputs, lead_shape):
    results = lax.map(lambda items: merge_one(*items), tuple((flatten_nodes(item) for item in inputs)))
    return [item.reshape(lead_shape + item.shape[1:]) for item in results]

def reference(skeleton, generator, skeleton_lists, upper_lists):
    skel_blocks = skeleton.reshape(BANDS, N_TX, R, N_TY, R).transpose(0, 1, 3, 2, 4)
    gen_blocks = generator.reshape(BANDS, N_TX, R, N_TY, R).transpose(0, 1, 3, 2, 4)
    order_low = skeleton_lists.reshape(BANDS, N_TY, 2, NODE_X, R).transpose(0, 3, 1, 2, 4).reshape(BANDS, NODE_X, N_TY, 2 * R).astype(jnp.int32)
    factor_one, panel_one, schur_one, gen_one = run_level((skel_blocks[:, :NODE_X], skel_blocks[:, NODE_X:], gen_blocks[:, :NODE_X], gen_blocks[:, NODE_X:], order_low), (BANDS, NODE_X, N_TY))
    order_high = upper_lists.reshape(BANDS, 2, NODE_Y, 2, NODE_X, R // 2).transpose(0, 4, 2, 1, 3, 5).reshape(BANDS, NODE_X, NODE_Y, 2 * R).astype(jnp.int32)
    factor_two, panel_two, schur_two, gen_two = run_level((schur_one[:, :, :NODE_Y], schur_one[:, :, NODE_Y:], gen_one[:, :, :NODE_Y], gen_one[:, :, NODE_Y:], order_high), (BANDS, NODE_X, NODE_Y))

    def layout_low(array_in):
        return array_in.reshape(BANDS, NODE_X, N_TY, R, 2, R // 2).transpose(0, 4, 1, 3, 2, 5).reshape(BANDS, N_TX * R, N_TY * R // 2)

    def layout_high(array_in):
        return array_in.reshape(BANDS, NODE_X, NODE_Y, R, 2, 2, R // 4).transpose(0, 5, 1, 3, 4, 2, 6).reshape(BANDS, N_TX * R, N_TY * R // 4)
    return (layout_low(factor_one), layout_low(panel_one), layout_high(factor_two), layout_high(panel_two), layout_high(schur_two))
```

```python
import jax
import jax.numpy as jnp
from jax import lax
from jax.experimental import pallas as pl
from jax.experimental.pallas import tpu as pltpu
from jax.sharding import PartitionSpec as P

F32 = jnp.float32
BF = jnp.bfloat16
R = 512
H = 256
T = 128
LIMIT = 56 << 20


def split2(x):
    hi = x.astype(BF)
    return hi, (x - hi.astype(F32)).astype(BF)


def split3(x):
    hi = x.astype(BF)
    rest = x - hi.astype(F32)
    mid = rest.astype(BF)
    return hi, mid, (rest - mid.astype(F32)).astype(BF)


def dot(a, b):
    return jnp.dot(a, b, preferred_element_type=F32)


def dot_tn(a, b):
    return lax.dot_general(a, b, (((0,), (0,)), ((), ())), preferred_element_type=F32)


def dot_nt(a, b):
    return lax.dot_general(a, b, (((1,), (1,)), ((), ())), preferred_element_type=F32)


def iota(shape, axis):
    return lax.broadcasted_iota(jnp.int32, shape, axis)


def pack_store(src, out):
    out[0:H, 0:H] = src[H:R, 0:H]
    rows, cols = iota((H, H), 0), iota((H, H), 1)
    first = src[0:H, 0:H]
    out[0:H, H:R] = jnp.where(rows >= cols, src[H:R, H:R], first)
    diag = jnp.sum(jnp.where(rows == cols, first, 0.0), axis=0, keepdims=True)
    out[H : H + 8, 0:H] = jnp.broadcast_to(diag, (8, H))
    out[H : H + 8, H:R] = jnp.zeros((8, H), F32)


def unpack_store(packed, out, base):
    low = packed[0:H, 0:H]
    mixed = packed[0:H, H:R]
    mixed_t = mixed.T
    rows, cols = iota((H, H), 0), iota((H, H), 1)
    diag = jnp.broadcast_to(packed[H : H + 1, 0:H], (H, H))
    first = jnp.where(rows < cols, mixed, mixed_t)
    out[base : base + H, 0:H] = jnp.where(rows == cols, diag, first)
    out[base : base + H, H:R] = low.T
    out[base + H : base + R, 0:H] = low
    out[base + H : base + R, H:R] = jnp.where(rows >= cols, mixed, mixed_t)


def pack_kernel(src, out):
    pack_store(src, out)


def pack(block):
    return pl.pallas_call(
        pack_kernel,
        out_shape=jax.ShapeDtypeStruct((H + 8, R), F32),
        compiler_params=pltpu.CompilerParams(vmem_limit_bytes=LIMIT),
        cost_estimate=pl.CostEstimate(flops=1 << 20, bytes_accessed=3 << 19, transcendentals=0),
        name="pack",
    )(block)


def gather_rows(order, source, target, count):
    def step(i, carry):
        for t in range(8):
            u = i * 8 + t
            target[pl.ds(u, 1), :] = source[pl.ds(order[u], 1), :]
        return carry

    lax.fori_loop(0, count // 8, step, 0)


def side_column(order_row, start):
    return jnp.broadcast_to((order_row[0:1, start : start + T] >> 9).astype(F32), (T, T)).T


def couple_kernel(order, order_row, own, other, main, tail, parent, stack, picked, hi, lo, sem):
    first = pltpu.make_async_copy(own, stack.at[0:R], sem.at[0])
    second = pltpu.make_async_copy(other, stack.at[R : 2 * R], sem.at[1])
    first.start()
    second.start()
    first.wait()
    second.wait()
    gather_rows(order, stack, picked, 2 * R)
    h, l = split2(picked[...])
    hi[...] = h
    lo[...] = l
    parent[...] = picked[R:, :]
    side_row = (order_row[...] >> 9).astype(F32)
    for i in range(8):
        rows = slice(i * T, i * T + T)
        start = 0 if i < 4 else R
        cols = slice(start, 2 * R)
        value = dot_nt(hi[rows], hi[cols]) + dot_nt(hi[rows], lo[cols]) + dot_nt(lo[rows], hi[cols])
        side = side_column(order_row, i * T)[:, 0:1]
        value = jnp.where(side != side_row[:, cols], value, 0.0)
        if i < 4:
            main[rows, :] = value
        else:
            tail[(i - 4) * T : (i - 4) * T + T, :] = value


def couple(order, own, other):
    any_spec = pl.BlockSpec(memory_space=pl.ANY)
    vmem = pl.BlockSpec(memory_space=pltpu.VMEM)
    return pl.pallas_call(
        couple_kernel,
        in_specs=[pl.BlockSpec(memory_space=pltpu.SMEM), vmem, any_spec, any_spec],
        out_shape=(
            jax.ShapeDtypeStruct((R, 2 * R), F32),
            jax.ShapeDtypeStruct((R, R), F32),
            jax.ShapeDtypeStruct((R, R), F32),
        ),
        scratch_shapes=[
            pltpu.VMEM((2 * R, R), F32),
            pltpu.VMEM((2 * R, R), F32),
            pltpu.VMEM((2 * R, R), BF),
            pltpu.VMEM((2 * R, R), BF),
            pltpu.SemaphoreType.DMA((2,)),
        ],
        compiler_params=pltpu.CompilerParams(vmem_limit_bytes=LIMIT),
        cost_estimate=pl.CostEstimate(flops=3 << 30, bytes_accessed=6 << 20, transcendentals=0),
        name="couple",
    )(order, order.reshape(1, 2 * R), own, other)


def factor_block(work):
    for s in range(16):
        at = 8 * s
        strip = work[at : at + 8, :]
        lines = [jnp.broadcast_to(strip[i : i + 1, :], (8, 2 * T)) for i in range(8)]
        small = {}
        for i in range(8):
            for j in range(i + 1):
                small[i, j] = jnp.broadcast_to(strip[j : j + 1, at + i : at + i + 1], (8, T))
        rows = iota((8, 2 * T), 0)
        out = None
        for j in range(8):
            inv = lax.rsqrt(small[j, j])
            line = lines[j] * jnp.concatenate([inv, inv], 1)
            out = line if out is None else jnp.where(rows == j, line, out)
            mult = {i: small[i, j] * inv for i in range(j + 1, 8)}
            for i in range(j + 1, 8):
                for k in range(j + 1, i + 1):
                    small[i, k] = small[i, k] - mult[i] * mult[k]
                lines[i] = lines[i] - jnp.concatenate([mult[i], mult[i]], 1) * line
        work[at : at + 8, :] = out
        if s < 15:
            h, m, l = split3(out)
            left = jnp.concatenate([h, h, m, h, m, l], 0)
            right = jnp.concatenate([h, m, h, l, m, h], 0)
            work[at + 8 :, :] = work[at + 8 :, :] - dot_tn(left[:, at + 8 : T], right)


def arrange(order, order_row, stack, picked, main, tail, area, kept):
    gather_rows(order, stack, picked, 2 * R)
    side_row = (order_row[...] >> 9).astype(F32)
    local = jnp.broadcast_to(order_row[...] & (R - 1), (R, 2 * R))
    hot = (iota((R, 2 * R), 0) == local).astype(F32).astype(BF)
    for i in range(8):
        rows = slice(i * T, i * T + T)
        start = 0 if i < 4 else R
        a, b, c = split3(picked[rows, :])
        value = dot(a, hot[:, start:]) + dot(b, hot[:, start:]) + dot(c, hot[:, start:])
        side = side_column(order_row, i * T)[:, 0:1]
        same = side == side_row[:, start:]
        if i < 4:
            area[rows, :] = jnp.where(same, value, main[rows, :])
        else:
            out_rows = slice((i - 4) * T, (i - 4) * T + T)
            kept[out_rows, :] = jnp.where(same, value, tail[out_rows, :])


def eliminate(area, factor, up_hi, up_lo, low_hi, low_lo, panel, work):
    eye = (iota((T, T), 0) == iota((T, T), 1)).astype(F32)
    upper = iota((T, T), 0) <= iota((T, T), 1)
    for k in range(4):
        o = k * T
        e = o + T
        block = area[o:e, o:]
        if k:
            block = block - (
                dot(low_hi[o:e, :o], up_hi[:o, o:])
                + dot(low_hi[o:e, :o], up_lo[:o, o:])
                + dot(low_lo[o:e, :o], up_hi[:o, o:])
            )
        work[:, :T] = block[:, :T]
        work[:, T:] = eye
        factor_block(work)
        inv_hi, inv_lo = split2(work[:, T:])
        rest_hi, rest_lo = split2(block[:, T:])
        solved = dot(inv_hi, rest_hi) + dot(inv_hi, rest_lo) + dot(inv_lo, rest_hi)
        solved_hi, solved_lo = split2(solved)
        up_hi[o:e, e:] = solved_hi
        up_lo[o:e, e:] = solved_lo
        panel[o:e, :] = solved[:, R - e :]
        factor[o:e, o:e] = jnp.where(upper, work[:, :T], 0.0).T
        for i in range(k + 1, 4):
            b = slice(i * T, i * T + T)
            factor[o:e, b] = jnp.zeros((T, T), F32)
            turned = solved[:, (i - k - 1) * T : (i - k) * T].T
            factor[b, o:e] = turned
            t_hi, t_lo = split2(turned)
            low_hi[b, o:e] = t_hi
            low_lo[b, o:e] = t_lo


def load_pair(own, packed, stack, sem):
    copy = pltpu.make_async_copy(own, stack.at[0:R], sem.at[0])
    copy.start()
    unpack_store(packed, stack, R)
    copy.wait()


def low_kernel(order, place, order_row, own, packed, main, tail, f_out, p_out, s_out, k_out, stack, picked, area, kept,
               factor, panel, up_hi, up_lo, low_hi, low_lo, work, sem):
    load_pair(own, packed, stack, sem)
    arrange(order, order_row, stack, picked, main, tail, area, kept)
    eliminate(area, factor, up_hi, up_lo, low_hi, low_lo, panel, work)
    p_hi, p_lo = up_hi[:, R:], up_lo[:, R:]
    s_out[...] = kept[...] - (dot_tn(p_hi, p_hi) + dot_tn(p_hi, p_lo) + dot_tn(p_lo, p_hi))
    pack_store(s_out, k_out)
    cols = pl.ds(pl.multiple_of(place[0] * H, H), H)
    f_out[...] = factor[:, cols]
    p_out[...] = panel[:, cols]


def high_kernel(order, place, order_row, own, packed, main, tail, f_out, p_out, s_out, stack, picked, area, kept,
                factor, panel, up_hi, up_lo, low_hi, low_lo, work, sem):
    load_pair(own, packed, stack, sem)
    arrange(order, order_row, stack, picked, main, tail, area, kept)
    eliminate(area, factor, up_hi, up_lo, low_hi, low_lo, panel, work)
    cols = pl.ds(pl.multiple_of(place[0] * T, T), T)
    mine = panel[:, cols]
    m_hi, m_lo = split2(mine)
    p_hi, p_lo = up_hi[:, R:], up_lo[:, R:]
    s_out[...] = kept[:, cols] - (dot_tn(p_hi, m_hi) + dot_tn(p_hi, m_lo) + dot_tn(p_lo, m_hi))
    f_out[...] = factor[:, cols]
    p_out[...] = mine


def level(kernel, name, out_shapes, order, place, own, packed, main, tail):
    any_spec = pl.BlockSpec(memory_space=pl.ANY)
    vmem = pl.BlockSpec(memory_space=pltpu.VMEM)
    smem = pl.BlockSpec(memory_space=pltpu.SMEM)
    return pl.pallas_call(
        kernel,
        in_specs=[smem, smem, vmem, any_spec, vmem, vmem, vmem],
        out_shape=tuple(jax.ShapeDtypeStruct(s, F32) for s in out_shapes),
        scratch_shapes=[
            pltpu.VMEM((2 * R, R), F32),
            pltpu.VMEM((2 * R, R), F32),
            pltpu.VMEM((R, 2 * R), F32),
            pltpu.VMEM((R, R), F32),
            pltpu.VMEM((R, R), F32),
            pltpu.VMEM((R, R), F32),
            pltpu.VMEM((R, 2 * R), BF),
            pltpu.VMEM((R, 2 * R), BF),
            pltpu.VMEM((R, R), BF),
            pltpu.VMEM((R, R), BF),
            pltpu.VMEM((T, 2 * T), F32),
            pltpu.SemaphoreType.DMA((1,)),
        ],
        compiler_params=pltpu.CompilerParams(vmem_limit_bytes=LIMIT),
        cost_estimate=pl.CostEstimate(flops=30 << 30, bytes_accessed=10 << 20, transcendentals=0),
        name=name,
    )(order, place, order.reshape(1, 2 * R), own, packed, main, tail)


def swap(value, axis):
    count = lax.axis_size(axis)
    return lax.ppermute(value, axis, [(i, (i + count // 2) % count) for i in range(count)])


def ordered(mine, theirs, parity):
    return jnp.where(parity == 0, jnp.concatenate((mine, theirs)), jnp.concatenate((theirs, mine)))


def body(skeleton, generator, skeleton_lists, upper_lists):
    tx_parity = lax.axis_index("tx") // (lax.axis_size("tx") // 2)
    ty_parity = lax.axis_index("ty") // (lax.axis_size("ty") // 2)
    block, gen = skeleton[0], generator[0]
    lists = jnp.concatenate((skeleton_lists[0, 0], upper_lists[0, 0]))
    got_lists = swap(lists, "tx")
    got_gen = swap(gen, "tx")
    got_packed = swap(pack(block), "tx")
    order_low = ordered(lists[:R], got_lists[:R], tx_parity) ^ (tx_parity * R)
    upper_own = ordered(lists[R:], got_lists[R:], tx_parity)
    upper_oth = swap(upper_own, "ty")
    order_high = ordered(upper_own, upper_oth, ty_parity) ^ (ty_parity * R)
    low_place = jnp.full((1,), tx_parity, jnp.int32)
    high_place = jnp.full((1,), 2 * ty_parity + tx_parity, jnp.int32)

    main, tail, parent = couple(order_low, gen, got_gen)
    oth_parent = swap(parent, "ty")
    factor_low, panel_low, schur, packed = level(
        low_kernel, "low", ((R, H), (R, H), (R, R), (H + 8, R)), order_low, low_place, block, got_packed, main, tail
    )
    oth_packed = swap(packed, "ty")
    main_high, tail_high, _ = couple(order_high, parent, oth_parent)
    factor_high, panel_high, schur_high = level(
        high_kernel, "high", ((R, T), (R, T), (R, T)), order_high, high_place, schur, oth_packed, main_high, tail_high
    )
    return factor_low[None], panel_low[None], factor_high[None], panel_high[None], schur_high[None]


def solution(mesh):
    spec = P(None, "tx", "ty")
    lists = P(None, "ty", "tx")
    return jax.shard_map(
        body, mesh=mesh, in_specs=(spec, spec, lists, lists), out_specs=(spec,) * 5, check_vma=False
    )
```

```python
import jax
import jax.numpy as jnp
from jax import lax
from jax.experimental import pallas as pl
from jax.experimental.pallas import tpu as pltpu
from jax.sharding import PartitionSpec as P

F32 = jnp.float32
BF = jnp.bfloat16
R = 512
H = 256
T = 128
LIMIT = 56 << 20


def split2(x):
    hi = x.astype(BF)
    return hi, (x - hi.astype(F32)).astype(BF)


def split3(x):
    hi = x.astype(BF)
    rest = x - hi.astype(F32)
    mid = rest.astype(BF)
    return hi, mid, (rest - mid.astype(F32)).astype(BF)


def dot(a, b):
    return jnp.dot(a, b, preferred_element_type=F32)


def dot_tn(a, b):
    return lax.dot_general(a, b, (((0,), (0,)), ((), ())), preferred_element_type=F32)


def dot_nt(a, b):
    return lax.dot_general(a, b, (((1,), (1,)), ((), ())), preferred_element_type=F32)


def iota(shape, axis):
    return lax.broadcasted_iota(jnp.int32, shape, axis)


def pack_store(src, out):
    out[0:H, 0:H] = src[H:R, 0:H]
    rows, cols = iota((H, H), 0), iota((H, H), 1)
    first = src[0:H, 0:H]
    out[0:H, H:R] = jnp.where(rows >= cols, src[H:R, H:R], first)
    diag = jnp.sum(jnp.where(rows == cols, first, 0.0), axis=0, keepdims=True)
    out[H : H + 8, 0:H] = jnp.broadcast_to(diag, (8, H))
    out[H : H + 8, H:R] = jnp.zeros((8, H), F32)


def unpack_store(packed, out, base):
    low = packed[0:H, 0:H]
    mixed = packed[0:H, H:R]
    mixed_t = mixed.T
    rows, cols = iota((H, H), 0), iota((H, H), 1)
    diag = jnp.broadcast_to(packed[H : H + 1, 0:H], (H, H))
    first = jnp.where(rows < cols, mixed, mixed_t)
    out[base : base + H, 0:H] = jnp.where(rows == cols, diag, first)
    out[base : base + H, H:R] = low.T
    out[base + H : base + R, 0:H] = low
    out[base + H : base + R, H:R] = jnp.where(rows >= cols, mixed, mixed_t)


def pack_kernel(src, out):
    pack_store(src, out)


def pack(block):
    return pl.pallas_call(
        pack_kernel,
        out_shape=jax.ShapeDtypeStruct((H + 8, R), F32),
        compiler_params=pltpu.CompilerParams(vmem_limit_bytes=LIMIT),
        cost_estimate=pl.CostEstimate(flops=1 << 20, bytes_accessed=3 << 19, transcendentals=0),
        name="pack",
    )(block)


def index_column(order_row, start):
    row = order_row[0:1, start : start + T].astype(F32)
    return jnp.broadcast_to(row, (T, T)).T


def fill_rows_hot(order_row, out, base, width):
    for i in range(8):
        col = index_column(order_row, i * T)
        for c in range(width // T):
            lane = (iota((T, T), 1) + (base + c * T)).astype(F32)
            out[i * T : i * T + T, c * T : c * T + T] = jnp.where(col == lane, 1.0, 0.0).astype(BF)


def fill_cols_hot(order_row, out, base):
    order = jnp.broadcast_to(order_row[...], (R, 2 * R))
    out[...] = jnp.where(iota((R, 2 * R), 0) + base == order, 1.0, 0.0).astype(BF)


def spread(block, rows_hot, cols_hot, row_offset):
    parts = [dot(piece, cols_hot[...]).astype(BF) for piece in split3(block)]
    cols = slice(row_offset, row_offset + R)
    main = sum(dot(rows_hot[:, cols], part[:, :R]) for part in parts)
    tail = sum(dot(rows_hot[R:, cols], part[:, R:]) for part in parts)
    return main, tail


def early_kernel(order_row, own_gen, oth_gen, own, main, tail, parent, rows_hot, cols_hot, hi, lo):
    fill_rows_hot(order_row, rows_hot, 0, 2 * R)
    own_parts, oth_parts = split3(own_gen[...]), split3(oth_gen[...])
    for i, out in ((0, hi), (1, lo)):
        out[...] = (dot(rows_hot[:, :R], own_parts[i]) + dot(rows_hot[:, R:], oth_parts[i])).astype(BF)
    rest = dot(rows_hot[R:, :R], own_parts[2]) + dot(rows_hot[R:, R:], oth_parts[2])
    parent[...] = hi[R:].astype(F32) + lo[R:].astype(F32) + rest
    fill_cols_hot(order_row, cols_hot, 0)
    own_main, own_tail = spread(own[...], rows_hot, cols_hot, 0)
    main[...] = own_main
    tail[...] = own_tail
    side_row = jnp.where(order_row[...] >= R, 1.0, 0.0)
    couple_main = dot_nt(hi[...], hi[:R]) + dot_nt(hi[...], lo[:R]) + dot_nt(lo[...], hi[:R])
    couple_tail = dot_nt(hi[R:], hi[R:]) + dot_nt(hi[R:], lo[R:]) + dot_nt(lo[R:], hi[R:])
    for i in range(8):
        side = jnp.where(index_column(order_row, i * T)[:, 0:1] >= R, 1.0, 0.0)
        rows = slice(i * T, i * T + T)
        main[rows, :] = main[rows, :] + jnp.where(side != side_row[:, :R], couple_main[rows], 0.0)
        if i >= 4:
            low = slice((i - 4) * T, (i - 4) * T + T)
            tail[low, :] = tail[low, :] + jnp.where(side != side_row[:, R:], couple_tail[low], 0.0)


def early(order_row, own_gen, oth_gen, own):
    vmem = pl.BlockSpec(memory_space=pltpu.VMEM)
    return pl.pallas_call(
        early_kernel,
        in_specs=[vmem] * 4,
        out_shape=(
            jax.ShapeDtypeStruct((2 * R, R), F32),
            jax.ShapeDtypeStruct((R, R), F32),
            jax.ShapeDtypeStruct((R, R), F32),
        ),
        scratch_shapes=[
            pltpu.VMEM((2 * R, 2 * R), BF),
            pltpu.VMEM((R, 2 * R), BF),
            pltpu.VMEM((2 * R, R), BF),
            pltpu.VMEM((2 * R, R), BF),
        ],
        compiler_params=pltpu.CompilerParams(vmem_limit_bytes=LIMIT),
        cost_estimate=pl.CostEstimate(flops=10 << 30, bytes_accessed=6 << 20, transcendentals=0),
        name="early",
    )(order_row, own_gen, oth_gen, own)


def twice(x):
    return jnp.concatenate([x, x], 1)


def lane(block, at):
    return jnp.broadcast_to(block[:, at : at + 1], (8, T))


def factor_block(work):
    strips = 8
    rows = iota((8, 2 * T), 0)
    for base in range(0, T, 8 * strips):
        group = [work[base + 8 * t : base + 8 * t + 8, :] for t in range(strips)]
        outs = []
        following = None
        for s in range(strips):
            at = base + 8 * s
            strip = group[s]
            lines = [jnp.broadcast_to(strip[i : i + 1, :], (8, 2 * T)) for i in range(8)]
            own = following if following is not None else [lane(strip, at + k) for k in range(8)]
            small = {(i, k): jnp.broadcast_to(own[k][i : i + 1, :], (8, T)) for i in range(8) for k in range(i + 1)}
            below = {(t, k): lane(group[t], at + k) for t in range(s + 1, strips) for k in range(8)}
            following = [lane(group[s + 1], at + 8 + k) for k in range(8)] if s + 1 < strips else None
            out = None
            for j in range(8):
                inv = lax.rsqrt(small[j, j])
                line = lines[j] * twice(inv)
                out = line if out is None else jnp.where(rows == j, line, out)
                mult = {i: small[i, j] * inv for i in range(j + 1, 8)}
                for i in range(j + 1, 8):
                    for k in range(j + 1, i + 1):
                        small[i, k] = small[i, k] - mult[i] * mult[k]
                    lines[i] = lines[i] - twice(mult[i]) * line
                for t in range(s + 1, strips):
                    m = below[t, j] * inv
                    group[t] = group[t] - twice(m) * line
                    for k in range(j + 1, 8):
                        below[t, k] = below[t, k] - m * mult[k]
                    if t == s + 1:
                        for k in range(8):
                            following[k] = following[k] - m * jnp.broadcast_to(m[k : k + 1, :], (8, T))
            work[at : at + 8, :] = out
            outs.append(out)
        end = base + 8 * strips
        if end < T:
            h, m, l = split3(jnp.concatenate(outs, 0))
            left = jnp.concatenate([h, h, m, h, m, l], 0)
            right = jnp.concatenate([h, m, h, l, m, h], 0)
            work[end:, :] = work[end:, :] - dot_tn(left[:, end:T], right)


def product(a_hi, a_lo, b_hi, b_lo):
    return dot_nt(a_hi, b_hi) + dot_nt(a_hi, b_lo) + dot_nt(a_lo, b_hi)


def eliminate(order_row, packed, main, tail, factor, area, kept, rows_hot, cols_hot, full, hi, lo, work):
    unpack_store(packed, full, 0)
    fill_rows_hot(order_row, rows_hot, R, R)
    fill_cols_hot(order_row, cols_hot, R)
    oth_main, oth_tail = spread(full[...], rows_hot, cols_hot, 0)
    area[...] = main[...] + oth_main
    kept[...] = tail[...] + oth_tail
    eye = (iota((T, T), 0) == iota((T, T), 1)).astype(F32)
    upper = iota((T, T), 0) <= iota((T, T), 1)
    for k in range(4):
        o = k * T
        e = o + T
        diag = area[o:e, o:e]
        rest = area[e:, o:e]
        if k:
            diag = diag - product(hi[o:e, :o], lo[o:e, :o], hi[o:e, :o], lo[o:e, :o])
            rest = rest - product(hi[e:, :o], lo[e:, :o], hi[o:e, :o], lo[o:e, :o])
        slot = work.at[k]
        slot[:, :T] = diag
        slot[:, T:] = eye
        factor_block(slot)
        inv_hi, inv_lo = split2(slot[:, T:])
        rest_hi, rest_lo = split2(rest)
        solved = product(rest_hi, rest_lo, inv_hi, inv_lo)
        s_hi, s_lo = split2(solved)
        hi[e:, o:e] = s_hi
        lo[e:, o:e] = s_lo
        factor[o:e, o:e] = jnp.where(upper, slot[:, :T], 0.0).T
        if e < R:
            factor[e:, o:e] = solved[: R - e]
            factor[o:e, e:] = jnp.zeros((T, R - e), F32)
        area[R:, o:e] = solved[R - e :]


def low_kernel(place, order_row, packed, main, tail, f_out, p_out, s_out, k_out,
               factor, area, kept, rows_hot, cols_hot, full, hi, lo, work):
    eliminate(order_row, packed, main, tail, factor, area, kept, rows_hot, cols_hot, full, hi, lo, work)
    s_out[...] = kept[...] - product(hi[R:], lo[R:], hi[R:], lo[R:])
    pack_store(s_out, k_out)
    at = pl.multiple_of(place[0] * H, H)
    f_out[...] = factor[:, pl.ds(at, H)]
    p_out[...] = area[pl.ds(R + at, H), :].T


def high_kernel(place, order_row, packed, main, tail, f_out, p_out, s_out,
                factor, area, kept, rows_hot, cols_hot, full, hi, lo, work):
    eliminate(order_row, packed, main, tail, factor, area, kept, rows_hot, cols_hot, full, hi, lo, work)
    at = pl.multiple_of(place[0] * T, T)
    mine = pl.ds(R + at, T)
    s_out[...] = kept[:, pl.ds(at, T)] - product(hi[R:], lo[R:], hi[mine, :], lo[mine, :])
    f_out[...] = factor[:, pl.ds(at, T)]
    p_out[...] = area[mine, :].T


def level(kernel, name, out_shapes, order_row, place, packed, main, tail):
    vmem = pl.BlockSpec(memory_space=pltpu.VMEM)
    smem = pl.BlockSpec(memory_space=pltpu.SMEM)
    return pl.pallas_call(
        kernel,
        in_specs=[smem, vmem, vmem, vmem, vmem],
        out_shape=tuple(jax.ShapeDtypeStruct(s, F32) for s in out_shapes),
        scratch_shapes=[
            pltpu.VMEM((R, R), F32),
            pltpu.VMEM((2 * R, R), F32),
            pltpu.VMEM((R, R), F32),
            pltpu.VMEM((2 * R, R), BF),
            pltpu.VMEM((R, 2 * R), BF),
            pltpu.VMEM((R, R), F32),
            pltpu.VMEM((2 * R, R), BF),
            pltpu.VMEM((2 * R, R), BF),
            pltpu.VMEM((4, T, 2 * T), F32),
        ],
        compiler_params=pltpu.CompilerParams(vmem_limit_bytes=LIMIT),
        cost_estimate=pl.CostEstimate(flops=30 << 30, bytes_accessed=10 << 20, transcendentals=0),
        name=name,
    )(place, order_row, packed, main, tail)


def swap(value, axis):
    count = lax.axis_size(axis)
    return lax.ppermute(value, axis, [(i, (i + count // 2) % count) for i in range(count)])


def ordered(mine, theirs, parity):
    return jnp.where(parity == 0, jnp.concatenate((mine, theirs)), jnp.concatenate((theirs, mine)))


def body(skeleton, generator, skeleton_lists, upper_lists):
    tx_parity = lax.axis_index("tx") // (lax.axis_size("tx") // 2)
    ty_parity = lax.axis_index("ty") // (lax.axis_size("ty") // 2)
    block, gen = skeleton[0], generator[0]
    mine_low, mine_up = skeleton_lists[0, 0], upper_lists[0, 0]
    got_low = swap(mine_low, "tx")
    got_up = swap(mine_up, "tx")
    got_gen = swap(gen, "tx")
    got_packed = swap(pack(block), "tx")
    order_low = (ordered(mine_low, got_low, tx_parity) ^ (tx_parity * R)).reshape(1, 2 * R)
    upper_own = ordered(mine_up, got_up, tx_parity)
    upper_oth = swap(upper_own, "ty")
    order_high = (ordered(upper_own, upper_oth, ty_parity) ^ (ty_parity * R)).reshape(1, 2 * R)
    low_place = jnp.full((1,), tx_parity, jnp.int32)
    high_place = jnp.full((1,), 2 * ty_parity + tx_parity, jnp.int32)

    main, tail, parent = early(order_low, gen, got_gen, block)
    oth_parent = swap(parent, "ty")
    main, order_high = lax.optimization_barrier((main, order_high))
    factor_low, panel_low, schur, packed = level(
        low_kernel, "low", ((R, H), (R, H), (R, R), (H + 8, R)), order_low, low_place, got_packed, main, tail
    )
    oth_packed = swap(packed, "ty")
    main_high, tail_high, _ = early(order_high, parent, oth_parent, schur)
    factor_high, panel_high, schur_high = level(
        high_kernel, "high", ((R, T), (R, T), (R, T)), order_high, high_place, oth_packed, main_high, tail_high
    )
    return factor_low[None], panel_low[None], factor_high[None], panel_high[None], schur_high[None]


def solution(mesh):
    spec = P(None, "tx", "ty")
    lists = P(None, "ty", "tx")
    return jax.shard_map(
        body, mesh=mesh, in_specs=(spec, spec, lists, lists), out_specs=(spec,) * 5, check_vma=False
    )
```

```python
import jax
import jax.numpy as jnp
from jax import lax
from jax.experimental import pallas as pl
from jax.experimental.pallas import tpu as pltpu
from jax.sharding import PartitionSpec as P

F32 = jnp.float32
BF = jnp.bfloat16
R = 512
H = 256
T = 128
LIMIT = 28 << 20


def split2(x):
    hi = x.astype(BF)
    return hi, (x - hi.astype(F32)).astype(BF)


def split3(x):
    hi = x.astype(BF)
    rest = x - hi.astype(F32)
    mid = rest.astype(BF)
    return hi, mid, (rest - mid.astype(F32)).astype(BF)


def dot(a, b):
    return jnp.dot(a, b, preferred_element_type=F32)


def dot_tn(a, b):
    return lax.dot_general(a, b, (((0,), (0,)), ((), ())), preferred_element_type=F32)


def dot_nt(a, b):
    return lax.dot_general(a, b, (((1,), (1,)), ((), ())), preferred_element_type=F32)


def iota(shape, axis):
    return lax.broadcasted_iota(jnp.int32, shape, axis)


def pack_store(src, out):
    out[0:H, 0:H] = src[H:R, 0:H]
    rows, cols = iota((H, H), 0), iota((H, H), 1)
    first = src[0:H, 0:H]
    out[0:H, H:R] = jnp.where(rows >= cols, src[H:R, H:R], first)
    diag = jnp.sum(jnp.where(rows == cols, first, 0.0), axis=0, keepdims=True)
    out[H : H + 8, 0:H] = jnp.broadcast_to(diag, (8, H))
    out[H : H + 8, H:R] = jnp.zeros((8, H), F32)


def unpack_store(packed, out, base):
    low = packed[0:H, 0:H]
    mixed = packed[0:H, H:R]
    mixed_t = mixed.T
    rows, cols = iota((H, H), 0), iota((H, H), 1)
    diag = jnp.broadcast_to(packed[H : H + 1, 0:H], (H, H))
    first = jnp.where(rows < cols, mixed, mixed_t)
    out[base : base + H, 0:H] = jnp.where(rows == cols, diag, first)
    out[base : base + H, H:R] = low.T
    out[base + H : base + R, 0:H] = low
    out[base + H : base + R, H:R] = jnp.where(rows >= cols, mixed, mixed_t)


def pack_kernel(src, out):
    pack_store(src, out)


def pack(block):
    return pl.pallas_call(
        pack_kernel,
        out_shape=jax.ShapeDtypeStruct((H + 8, R), F32),
        compiler_params=pltpu.CompilerParams(vmem_limit_bytes=LIMIT),
        cost_estimate=pl.CostEstimate(flops=1 << 20, bytes_accessed=3 << 19, transcendentals=0),
        name="pack",
    )(block)


def index_column(order_row, start):
    row = order_row[0:1, start : start + T].astype(F32)
    return jnp.broadcast_to(row, (T, T)).T


def fill_rows_hot(order_row, out, base, width, side=None):
    for i in range(8):
        col = index_column(order_row, i * T)
        if side is not None:
            side[i * T : i * T + T, :] = jnp.where(col >= R, 1.0, 0.0)
        for c in range(width // T):
            lane = (iota((T, T), 1) + (base + c * T)).astype(F32)
            out[i * T : i * T + T, c * T : c * T + T] = jnp.where(col == lane, 1.0, 0.0).astype(BF)


def fill_cols_hot(order_row, out, base):
    order = jnp.broadcast_to(order_row[...], (R, 2 * R))
    out[...] = jnp.where(iota((R, 2 * R), 0) + base == order, 1.0, 0.0).astype(BF)


def halves(step):
    def run(i, carry):
        step(pl.ds(pl.multiple_of(i * R, R), R))
        return carry

    lax.fori_loop(0, 2, run, 0)


def spread_columns(block, cols_hot, parts):
    for i, piece in enumerate(split2(block)):
        parts[i] = dot(piece, cols_hot[...]).astype(BF)


def early_kernel(order_row, own_gen, oth_gen, own, main, tail, *rest):
    parent = rest[0] if len(rest) == 7 else None
    rows_hot, cols_hot, hi, lo, parts, side = rest[-6:]
    fill_rows_hot(order_row, rows_hot, 0, 2 * R, side)
    fill_cols_hot(order_row, cols_hot, 0)
    own_parts, oth_parts = split3(own_gen[...]), split3(oth_gen[...])

    def pick(rows):
        for i, out in ((0, hi), (1, lo)):
            out[rows, :] = (dot(rows_hot[rows, :R], own_parts[i]) + dot(rows_hot[rows, R:], oth_parts[i])).astype(BF)

    halves(pick)
    if parent is not None:
        last = dot(rows_hot[R:, :R], own_parts[2]) + dot(rows_hot[R:, R:], oth_parts[2])
        parent[...] = hi[R:].astype(F32) + lo[R:].astype(F32) + last
    spread_columns(own[...], cols_hot, parts)
    side_row = jnp.where(order_row[...] >= R, 1.0, 0.0)

    def fill(rows, cols, out, out_rows):
        coupling = dot_nt(hi[rows, :], hi[cols]) + dot_nt(hi[rows, :], lo[cols]) + dot_nt(lo[rows, :], hi[cols])
        coupling = jnp.where(side[rows, 0:1] != side_row[:, cols], coupling, 0.0)
        out[out_rows, :] = coupling + dot(rows_hot[rows, :R], parts[0, :, cols]) + dot(rows_hot[rows, :R], parts[1, :, cols])

    halves(lambda rows: fill(rows, slice(0, R), main, rows))
    fill(slice(R, 2 * R), slice(R, 2 * R), tail, slice(0, R))


def early(order_row, own_gen, oth_gen, own, with_parent):
    vmem = pl.BlockSpec(memory_space=pltpu.VMEM)
    shapes = ((2 * R, R), (R, R)) + (((R, R),) if with_parent else ())
    return pl.pallas_call(
        early_kernel,
        in_specs=[vmem] * 4,
        out_shape=tuple(jax.ShapeDtypeStruct(s, F32) for s in shapes),
        scratch_shapes=[
            pltpu.VMEM((2 * R, 2 * R), BF),
            pltpu.VMEM((R, 2 * R), BF),
            pltpu.VMEM((2 * R, R), BF),
            pltpu.VMEM((2 * R, R), BF),
            pltpu.VMEM((2, R, 2 * R), BF),
            pltpu.VMEM((2 * R, T), F32),
        ],
        compiler_params=pltpu.CompilerParams(vmem_limit_bytes=LIMIT),
        cost_estimate=pl.CostEstimate(flops=10 << 30, bytes_accessed=6 << 20, transcendentals=0),
        name="early",
    )(order_row, own_gen, oth_gen, own)


def twice(x):
    return jnp.concatenate([x, x], 1)


def lane(block, at):
    return jnp.broadcast_to(block[:, at : at + 1], (8, T))


def factor_block(work):
    strips = 8
    rows = iota((8, 2 * T), 0)
    for base in range(0, T, 8 * strips):
        group = [work[base + 8 * t : base + 8 * t + 8, :] for t in range(strips)]
        outs = []
        following = None
        for s in range(strips):
            at = base + 8 * s
            strip = group[s]
            lines = [jnp.broadcast_to(strip[i : i + 1, :], (8, 2 * T)) for i in range(8)]
            own = following if following is not None else [lane(strip, at + k) for k in range(8)]
            small = {(i, k): jnp.broadcast_to(own[k][i : i + 1, :], (8, T)) for i in range(8) for k in range(i + 1)}
            below = {(t, k): lane(group[t], at + k) for t in range(s + 1, strips) for k in range(8)}
            following = [lane(group[s + 1], at + 8 + k) for k in range(8)] if s + 1 < strips else None
            out = None
            for j in range(8):
                inv = lax.rsqrt(small[j, j])
                line = lines[j] * twice(inv)
                out = line if out is None else jnp.where(rows == j, line, out)
                mult = {i: small[i, j] * inv for i in range(j + 1, 8)}
                for i in range(j + 1, 8):
                    for k in range(j + 1, i + 1):
                        small[i, k] = small[i, k] - mult[i] * mult[k]
                    lines[i] = lines[i] - twice(mult[i]) * line
                for t in range(s + 1, strips):
                    m = below[t, j] * inv
                    group[t] = group[t] - twice(m) * line
                    for k in range(j + 1, 8):
                        below[t, k] = below[t, k] - m * mult[k]
                    if t == s + 1:
                        for k in range(8):
                            following[k] = following[k] - m * jnp.broadcast_to(m[k : k + 1, :], (8, T))
            work[at : at + 8, :] = out
            outs.append(out)
        end = base + 8 * strips
        if end < T:
            h, m, l = split3(jnp.concatenate(outs, 0))
            left = jnp.concatenate([h, h, m, h, m, l], 0)
            right = jnp.concatenate([h, m, h, l, m, h], 0)
            work[end:, :] = work[end:, :] - dot_tn(left[:, end:T], right)


def product(a_hi, a_lo, b_hi, b_lo):
    return dot_nt(a_hi, b_hi) + dot_nt(a_hi, b_lo) + dot_nt(a_lo, b_hi)


def eliminate(order_row, packed, main, tail, factor, area, kept, rows_hot, cols_hot, parts, full, hi, lo, work):
    unpack_store(packed, full, 0)
    fill_rows_hot(order_row, rows_hot, R, R)
    fill_cols_hot(order_row, cols_hot, R)
    spread_columns(full[...], cols_hot, parts)

    def fill(rows):
        area[rows, :] = main[rows, :] + dot(rows_hot[rows, :], parts[0, :, :R]) + dot(rows_hot[rows, :], parts[1, :, :R])

    halves(fill)
    kept[...] = tail[...] + dot(rows_hot[R:, :], parts[0, :, R:]) + dot(rows_hot[R:, :], parts[1, :, R:])
    eye = (iota((T, T), 0) == iota((T, T), 1)).astype(F32)
    upper = iota((T, T), 0) <= iota((T, T), 1)
    for k in range(4):
        o = k * T
        e = o + T
        diag = area[o:e, o:e]
        rest = area[e:, o:e]
        if k:
            diag = diag - product(hi[o:e, :o], lo[o:e, :o], hi[o:e, :o], lo[o:e, :o])
            rest = rest - product(hi[e:, :o], lo[e:, :o], hi[o:e, :o], lo[o:e, :o])
        slot = work.at[k]
        slot[:, :T] = diag
        slot[:, T:] = eye
        factor_block(slot)
        inv_hi, inv_lo = split2(slot[:, T:])
        rest_hi, rest_lo = split2(rest)
        solved = product(rest_hi, rest_lo, inv_hi, inv_lo)
        s_hi, s_lo = split2(solved)
        hi[e:, o:e] = s_hi
        lo[e:, o:e] = s_lo
        factor[o:e, o:e] = jnp.where(upper, slot[:, :T], 0.0).T
        if e < R:
            factor[e:, o:e] = solved[: R - e]
            factor[o:e, e:] = jnp.zeros((T, R - e), F32)
        area[R:, o:e] = solved[R - e :]


def low_kernel(place, order_row, packed, main, tail, f_out, p_out, s_out, k_out,
               factor, area, kept, rows_hot, cols_hot, parts, full, hi, lo, work):
    eliminate(order_row, packed, main, tail, factor, area, kept, rows_hot, cols_hot, parts, full, hi, lo, work)
    s_out[...] = kept[...] - product(hi[R:], lo[R:], hi[R:], lo[R:])
    pack_store(s_out, k_out)
    at = pl.multiple_of(place[0] * H, H)
    f_out[...] = factor[:, pl.ds(at, H)]
    p_out[...] = area[pl.ds(R + at, H), :].T


def high_kernel(place, order_row, packed, main, tail, f_out, p_out, s_out,
                factor, area, kept, rows_hot, cols_hot, parts, full, hi, lo, work):
    eliminate(order_row, packed, main, tail, factor, area, kept, rows_hot, cols_hot, parts, full, hi, lo, work)
    at = pl.multiple_of(place[0] * T, T)
    mine = pl.ds(R + at, T)
    s_out[...] = kept[:, pl.ds(at, T)] - product(hi[R:], lo[R:], hi[mine, :], lo[mine, :])
    f_out[...] = factor[:, pl.ds(at, T)]
    p_out[...] = area[mine, :].T


def level(kernel, name, out_shapes, order_row, place, packed, main, tail):
    vmem = pl.BlockSpec(memory_space=pltpu.VMEM)
    smem = pl.BlockSpec(memory_space=pltpu.SMEM)
    return pl.pallas_call(
        kernel,
        in_specs=[smem, vmem, vmem, vmem, vmem],
        out_shape=tuple(jax.ShapeDtypeStruct(s, F32) for s in out_shapes),
        scratch_shapes=[
            pltpu.VMEM((R, R), F32),
            pltpu.VMEM((2 * R, R), F32),
            pltpu.VMEM((R, R), F32),
            pltpu.VMEM((2 * R, R), BF),
            pltpu.VMEM((R, 2 * R), BF),
            pltpu.VMEM((2, R, 2 * R), BF),
            pltpu.VMEM((R, R), F32),
            pltpu.VMEM((2 * R, R), BF),
            pltpu.VMEM((2 * R, R), BF),
            pltpu.VMEM((4, T, 2 * T), F32),
        ],
        compiler_params=pltpu.CompilerParams(vmem_limit_bytes=LIMIT),
        cost_estimate=pl.CostEstimate(flops=30 << 30, bytes_accessed=10 << 20, transcendentals=0),
        name=name,
    )(place, order_row, packed, main, tail)


def swap(value, axis):
    count = lax.axis_size(axis)
    return lax.ppermute(value, axis, [(i, (i + count // 2) % count) for i in range(count)])


def ordered(mine, theirs, parity):
    return jnp.where(parity == 0, jnp.concatenate((mine, theirs)), jnp.concatenate((theirs, mine)))


def body(skeleton, generator, skeleton_lists, upper_lists):
    tx_parity = lax.axis_index("tx") // (lax.axis_size("tx") // 2)
    ty_parity = lax.axis_index("ty") // (lax.axis_size("ty") // 2)
    block, gen = skeleton[0], generator[0]
    mine_low, mine_up = skeleton_lists[0, 0], upper_lists[0, 0]
    got_low = swap(mine_low, "tx")
    got_up = swap(mine_up, "tx")
    got_gen = swap(gen, "tx")
    got_packed = swap(pack(block), "tx")
    order_low = (ordered(mine_low, got_low, tx_parity) ^ (tx_parity * R)).reshape(1, 2 * R)
    upper_own = ordered(mine_up, got_up, tx_parity)
    upper_oth = swap(upper_own, "ty")
    order_high = (ordered(upper_own, upper_oth, ty_parity) ^ (ty_parity * R)).reshape(1, 2 * R)
    low_place = jnp.full((1,), tx_parity, jnp.int32)
    high_place = jnp.full((1,), 2 * ty_parity + tx_parity, jnp.int32)

    main, tail, parent = early(order_low, gen, got_gen, block, True)
    oth_parent = swap(parent, "ty")
    main, order_high = lax.optimization_barrier((main, order_high))
    factor_low, panel_low, schur, packed = level(
        low_kernel, "low", ((R, H), (R, H), (R, R), (H + 8, R)), order_low, low_place, got_packed, main, tail
    )
    oth_packed = swap(packed, "ty")
    main_high, tail_high = early(order_high, parent, oth_parent, schur, False)
    factor_high, panel_high, schur_high = level(
        high_kernel, "high", ((R, T), (R, T), (R, T)), order_high, high_place, oth_packed, main_high, tail_high
    )
    return factor_low[None], panel_low[None], factor_high[None], panel_high[None], schur_high[None]


def solution(mesh):
    spec = P(None, "tx", "ty")
    lists = P(None, "ty", "tx")
    return jax.shard_map(
        body, mesh=mesh, in_specs=(spec, spec, lists, lists), out_specs=(spec,) * 5, check_vma=False
    )
```

```python
import jax
import jax.numpy as jnp
from jax import lax
from jax.experimental import pallas as pl
from jax.experimental.pallas import tpu as pltpu
from jax.sharding import PartitionSpec as P

F32 = jnp.float32
BF = jnp.bfloat16
R = 512
H = 256
T = 128
LIMIT = 28 << 20


def split2(x):
    hi = x.astype(BF)
    return hi, (x - hi.astype(F32)).astype(BF)


def split3(x):
    hi = x.astype(BF)
    rest = x - hi.astype(F32)
    mid = rest.astype(BF)
    return hi, mid, (rest - mid.astype(F32)).astype(BF)


def dot(a, b):
    return jnp.dot(a, b, preferred_element_type=F32)


def dot_tn(a, b):
    return lax.dot_general(a, b, (((0,), (0,)), ((), ())), preferred_element_type=F32)


def dot_nt(a, b):
    return lax.dot_general(a, b, (((1,), (1,)), ((), ())), preferred_element_type=F32)


def iota(shape, axis):
    return lax.broadcasted_iota(jnp.int32, shape, axis)


def pack_store(src, out):
    out[0:H, 0:H] = src[H:R, 0:H]
    rows, cols = iota((H, H), 0), iota((H, H), 1)
    first = src[0:H, 0:H]
    out[0:H, H:R] = jnp.where(rows >= cols, src[H:R, H:R], first)
    diag = jnp.sum(jnp.where(rows == cols, first, 0.0), axis=0, keepdims=True)
    out[H : H + 8, 0:H] = jnp.broadcast_to(diag, (8, H))
    out[H : H + 8, H:R] = jnp.zeros((8, H), F32)


def unpack_store(packed, out, base):
    low = packed[0:H, 0:H]
    mixed = packed[0:H, H:R]
    mixed_t = mixed.T
    rows, cols = iota((H, H), 0), iota((H, H), 1)
    diag = jnp.broadcast_to(packed[H : H + 1, 0:H], (H, H))
    first = jnp.where(rows < cols, mixed, mixed_t)
    out[base : base + H, 0:H] = jnp.where(rows == cols, diag, first)
    out[base : base + H, H:R] = low.T
    out[base + H : base + R, 0:H] = low
    out[base + H : base + R, H:R] = jnp.where(rows >= cols, mixed, mixed_t)


def pack_kernel(src, out):
    pack_store(src, out)


def pack(block):
    return pl.pallas_call(
        pack_kernel,
        out_shape=jax.ShapeDtypeStruct((H + 8, R), F32),
        compiler_params=pltpu.CompilerParams(vmem_limit_bytes=LIMIT),
        cost_estimate=pl.CostEstimate(flops=1 << 20, bytes_accessed=3 << 19, transcendentals=0),
        name="pack",
    )(block)


def index_column(order_row, start):
    row = order_row[0:1, start : start + T].astype(F32)
    return jnp.broadcast_to(row, (T, T)).T


def fill_rows_hot(order_row, out, base, width, side=None):
    for i in range(8):
        col = index_column(order_row, i * T)
        if side is not None:
            side[i * T : i * T + T, :] = jnp.where(col >= R, 1.0, 0.0)
        for c in range(width // T):
            lane = (iota((T, T), 1) + (base + c * T)).astype(F32)
            out[i * T : i * T + T, c * T : c * T + T] = jnp.where(col == lane, 1.0, 0.0).astype(BF)


def fill_cols_hot(order_row, out, base):
    order = jnp.broadcast_to(order_row[...], (R, 2 * R))
    out[...] = jnp.where(iota((R, 2 * R), 0) + base == order, 1.0, 0.0).astype(BF)


def halves(step):
    def run(i, carry):
        step(pl.ds(pl.multiple_of(i * R, R), R))
        return carry

    lax.fori_loop(0, 2, run, 0)


def spread_columns(block, cols_hot, parts):
    for i, piece in enumerate(split2(block)):
        parts[i] = dot(piece, cols_hot[...]).astype(BF)


def own_kernel(order_row, gen, block, main, tail, g_hi, g_lo, *rest):
    parent = rest[0] if len(rest) == 4 else None
    rows_hot, cols_hot, parts = rest[-3:]
    fill_rows_hot(order_row, rows_hot, 0, R)
    fill_cols_hot(order_row, cols_hot, 0)
    pieces = split3(gen[...])

    def pick(rows):
        g_hi[rows, :] = dot(rows_hot[rows, :], pieces[0]).astype(BF)
        g_lo[rows, :] = dot(rows_hot[rows, :], pieces[1]).astype(BF)

    halves(pick)
    if parent is not None:
        parent[...] = g_hi[R:].astype(F32) + g_lo[R:].astype(F32) + dot(rows_hot[R:], pieces[2])
    spread_columns(block[...], cols_hot, parts)

    def fill(rows):
        main[rows, :] = dot(rows_hot[rows, :], parts[0, :, :R]) + dot(rows_hot[rows, :], parts[1, :, :R])

    halves(fill)
    tail[...] = dot(rows_hot[R:, :], parts[0, :, R:]) + dot(rows_hot[R:, :], parts[1, :, R:])


def couple_kernel(order_row, gen, main_in, tail_in, g_hi, g_lo, *rest):
    with_parent = len(rest) == 8
    parent_in = rest[0] if with_parent else None
    main, tail = rest[1:3] if with_parent else rest[:2]
    parent = rest[3] if with_parent else None
    rows_hot, hi, lo, side = rest[-4:]
    fill_rows_hot(order_row, rows_hot, R, R, side)
    pieces = split3(gen[...])

    def pick(rows):
        hi[rows, :] = (g_hi[rows, :].astype(F32) + dot(rows_hot[rows, :], pieces[0])).astype(BF)
        lo[rows, :] = (g_lo[rows, :].astype(F32) + dot(rows_hot[rows, :], pieces[1])).astype(BF)

    halves(pick)
    if with_parent:
        high, mid, low = (dot(rows_hot[R:], piece) for piece in pieces)
        parent[...] = parent_in[...] + (high + mid + low)
    side_row = jnp.where(order_row[...] >= R, 1.0, 0.0)

    def fill(rows, cols, before, out, out_rows):
        coupling = dot_nt(hi[rows, :], hi[cols]) + dot_nt(hi[rows, :], lo[cols]) + dot_nt(lo[rows, :], hi[cols])
        out[out_rows, :] = before[out_rows, :] + jnp.where(side[rows, 0:1] != side_row[:, cols], coupling, 0.0)

    halves(lambda rows: fill(rows, slice(0, R), main_in, main, rows))
    fill(slice(R, 2 * R), slice(R, 2 * R), tail_in, tail, slice(0, R))


def place_own(order_row, gen, block, with_parent):
    vmem = pl.BlockSpec(memory_space=pltpu.VMEM)
    shapes = [((2 * R, R), F32), ((R, R), F32), ((2 * R, R), BF), ((2 * R, R), BF)] + [((R, R), F32)] * with_parent
    return pl.pallas_call(
        own_kernel,
        in_specs=[vmem] * 3,
        out_shape=tuple(jax.ShapeDtypeStruct(*s) for s in shapes),
        scratch_shapes=[pltpu.VMEM((2 * R, R), BF), pltpu.VMEM((R, 2 * R), BF), pltpu.VMEM((2, R, 2 * R), BF)],
        compiler_params=pltpu.CompilerParams(vmem_limit_bytes=LIMIT),
        cost_estimate=pl.CostEstimate(flops=5 << 30, bytes_accessed=6 << 20, transcendentals=0),
        name="place_own",
    )(order_row, gen, block)


def couple(order_row, gen, own):
    vmem = pl.BlockSpec(memory_space=pltpu.VMEM)
    shapes = [(2 * R, R), (R, R)] + [(R, R)] * (len(own) == 5)
    return pl.pallas_call(
        couple_kernel,
        in_specs=[vmem] * (2 + len(own)),
        out_shape=tuple(jax.ShapeDtypeStruct(s, F32) for s in shapes),
        scratch_shapes=[pltpu.VMEM((2 * R, R), BF)] * 3 + [pltpu.VMEM((2 * R, T), F32)],
        compiler_params=pltpu.CompilerParams(vmem_limit_bytes=LIMIT),
        cost_estimate=pl.CostEstimate(flops=5 << 30, bytes_accessed=6 << 20, transcendentals=0),
        name="couple",
    )(order_row, gen, *own)


def twice(x):
    return jnp.concatenate([x, x], 1)


def lane(block, at):
    return jnp.broadcast_to(block[:, at : at + 1], (8, T))


def factor_block(work):
    strips = 8
    rows = iota((8, 2 * T), 0)
    for base in range(0, T, 8 * strips):
        group = [work[base + 8 * t : base + 8 * t + 8, :] for t in range(strips)]
        outs = []
        following = None
        for s in range(strips):
            at = base + 8 * s
            strip = group[s]
            lines = [jnp.broadcast_to(strip[i : i + 1, :], (8, 2 * T)) for i in range(8)]
            own = following if following is not None else [lane(strip, at + k) for k in range(8)]
            small = {(i, k): jnp.broadcast_to(own[k][i : i + 1, :], (8, T)) for i in range(8) for k in range(i + 1)}
            below = {(t, k): lane(group[t], at + k) for t in range(s + 1, strips) for k in range(8)}
            following = [lane(group[s + 1], at + 8 + k) for k in range(8)] if s + 1 < strips else None
            out = None
            for j in range(8):
                inv = lax.rsqrt(small[j, j])
                line = lines[j] * twice(inv)
                out = line if out is None else jnp.where(rows == j, line, out)
                mult = {i: small[i, j] * inv for i in range(j + 1, 8)}
                for i in range(j + 1, 8):
                    for k in range(j + 1, i + 1):
                        small[i, k] = small[i, k] - mult[i] * mult[k]
                    lines[i] = lines[i] - twice(mult[i]) * line
                for t in range(s + 1, strips):
                    m = below[t, j] * inv
                    group[t] = group[t] - twice(m) * line
                    for k in range(j + 1, 8):
                        below[t, k] = below[t, k] - m * mult[k]
                    if t == s + 1:
                        for k in range(8):
                            following[k] = following[k] - m * jnp.broadcast_to(m[k : k + 1, :], (8, T))
            work[at : at + 8, :] = out
            outs.append(out)
        end = base + 8 * strips
        if end < T:
            h, m, l = split3(jnp.concatenate(outs, 0))
            left = jnp.concatenate([h, h, m, h, m, l], 0)
            right = jnp.concatenate([h, m, h, l, m, h], 0)
            work[end:, :] = work[end:, :] - dot_tn(left[:, end:T], right)


def product(a_hi, a_lo, b_hi, b_lo):
    return dot_nt(a_hi, b_hi) + dot_nt(a_hi, b_lo) + dot_nt(a_lo, b_hi)


def eliminate(order_row, packed, main, tail, factor, area, kept, rows_hot, cols_hot, parts, full, hi, lo, work):
    unpack_store(packed, full, 0)
    fill_rows_hot(order_row, rows_hot, R, R)
    fill_cols_hot(order_row, cols_hot, R)
    spread_columns(full[...], cols_hot, parts)

    def fill(rows):
        area[rows, :] = main[rows, :] + dot(rows_hot[rows, :], parts[0, :, :R]) + dot(rows_hot[rows, :], parts[1, :, :R])

    halves(fill)
    kept[...] = tail[...] + dot(rows_hot[R:, :], parts[0, :, R:]) + dot(rows_hot[R:, :], parts[1, :, R:])
    eye = (iota((T, T), 0) == iota((T, T), 1)).astype(F32)
    upper = iota((T, T), 0) <= iota((T, T), 1)
    for k in range(4):
        o = k * T
        e = o + T
        diag = area[o:e, o:e]
        rest = area[e:, o:e]
        if k:
            diag = diag - product(hi[o:e, :o], lo[o:e, :o], hi[o:e, :o], lo[o:e, :o])
            rest = rest - product(hi[e:, :o], lo[e:, :o], hi[o:e, :o], lo[o:e, :o])
        slot = work.at[k]
        slot[:, :T] = diag
        slot[:, T:] = eye
        factor_block(slot)
        inv_hi, inv_lo = split2(slot[:, T:])
        rest_hi, rest_lo = split2(rest)
        solved = product(rest_hi, rest_lo, inv_hi, inv_lo)
        s_hi, s_lo = split2(solved)
        hi[e:, o:e] = s_hi
        lo[e:, o:e] = s_lo
        factor[o:e, o:e] = jnp.where(upper, slot[:, :T], 0.0).T
        if e < R:
            factor[e:, o:e] = solved[: R - e]
            factor[o:e, e:] = jnp.zeros((T, R - e), F32)
        area[R:, o:e] = solved[R - e :]


def low_kernel(place, order_row, packed, main, tail, f_out, p_out, s_out, k_out,
               factor, area, kept, rows_hot, cols_hot, parts, full, hi, lo, work):
    eliminate(order_row, packed, main, tail, factor, area, kept, rows_hot, cols_hot, parts, full, hi, lo, work)
    s_out[...] = kept[...] - product(hi[R:], lo[R:], hi[R:], lo[R:])
    pack_store(s_out, k_out)
    at = pl.multiple_of(place[0] * H, H)
    f_out[...] = factor[:, pl.ds(at, H)]
    p_out[...] = area[pl.ds(R + at, H), :].T


def high_kernel(place, order_row, packed, main, tail, f_out, p_out, s_out,
                factor, area, kept, rows_hot, cols_hot, parts, full, hi, lo, work):
    eliminate(order_row, packed, main, tail, factor, area, kept, rows_hot, cols_hot, parts, full, hi, lo, work)
    at = pl.multiple_of(place[0] * T, T)
    mine = pl.ds(R + at, T)
    s_out[...] = kept[:, pl.ds(at, T)] - product(hi[R:], lo[R:], hi[mine, :], lo[mine, :])
    f_out[...] = factor[:, pl.ds(at, T)]
    p_out[...] = area[mine, :].T


def level(kernel, name, out_shapes, order_row, place, packed, main, tail):
    vmem = pl.BlockSpec(memory_space=pltpu.VMEM)
    smem = pl.BlockSpec(memory_space=pltpu.SMEM)
    return pl.pallas_call(
        kernel,
        in_specs=[smem, vmem, vmem, vmem, vmem],
        out_shape=tuple(jax.ShapeDtypeStruct(s, F32) for s in out_shapes),
        scratch_shapes=[
            pltpu.VMEM((R, R), F32),
            pltpu.VMEM((2 * R, R), F32),
            pltpu.VMEM((R, R), F32),
            pltpu.VMEM((2 * R, R), BF),
            pltpu.VMEM((R, 2 * R), BF),
            pltpu.VMEM((2, R, 2 * R), BF),
            pltpu.VMEM((R, R), F32),
            pltpu.VMEM((2 * R, R), BF),
            pltpu.VMEM((2 * R, R), BF),
            pltpu.VMEM((4, T, 2 * T), F32),
        ],
        compiler_params=pltpu.CompilerParams(vmem_limit_bytes=LIMIT),
        cost_estimate=pl.CostEstimate(flops=30 << 30, bytes_accessed=10 << 20, transcendentals=0),
        name=name,
    )(place, order_row, packed, main, tail)


def swap(value, axis):
    count = lax.axis_size(axis)
    return lax.ppermute(value, axis, [(i, (i + count // 2) % count) for i in range(count)])


def ordered(mine, theirs, parity):
    return jnp.where(parity == 0, jnp.concatenate((mine, theirs)), jnp.concatenate((theirs, mine)))


def body(skeleton, generator, skeleton_lists, upper_lists):
    tx_parity = lax.axis_index("tx") // (lax.axis_size("tx") // 2)
    ty_parity = lax.axis_index("ty") // (lax.axis_size("ty") // 2)
    block, gen = skeleton[0], generator[0]
    lists = jnp.concatenate((skeleton_lists[0, 0], upper_lists[0, 0]))
    got_lists = swap(lists, "tx")
    sent_gen, sent_block = lax.optimization_barrier((gen, block, got_lists))[:2]
    got_gen = swap(sent_gen, "tx")
    got_packed = swap(pack(sent_block), "tx")
    order_low = (ordered(lists[:R], got_lists[:R], tx_parity) ^ (tx_parity * R)).reshape(1, 2 * R)
    upper_own = ordered(lists[R:], got_lists[R:], tx_parity)
    upper_oth = swap(upper_own, "ty")
    order_high = (ordered(upper_own, upper_oth, ty_parity) ^ (ty_parity * R)).reshape(1, 2 * R)
    low_place = jnp.full((1,), tx_parity, jnp.int32)
    high_place = jnp.full((1,), 2 * ty_parity + tx_parity, jnp.int32)

    own = place_own(order_low, gen, block, True)
    got_gen = lax.optimization_barrier((got_gen, own[0], order_high))[0]
    main, tail, parent = couple(order_low, got_gen, own)
    oth_parent = swap(parent, "ty")
    factor_low, panel_low, schur, packed = level(
        low_kernel, "low", ((R, H), (R, H), (R, R), (H + 8, R)), order_low, low_place, got_packed, main, tail
    )
    oth_packed = swap(packed, "ty")
    own_high = place_own(order_high, parent, schur, False)
    oth_parent = lax.optimization_barrier((oth_parent, own_high[0]))[0]
    main_high, tail_high = couple(order_high, oth_parent, own_high)
    factor_high, panel_high, schur_high = level(
        high_kernel, "high", ((R, T), (R, T), (R, T)), order_high, high_place, oth_packed, main_high, tail_high
    )
    return factor_low[None], panel_low[None], factor_high[None], panel_high[None], schur_high[None]


def solution(mesh):
    spec = P(None, "tx", "ty")
    lists = P(None, "ty", "tx")
    return jax.shard_map(
        body, mesh=mesh, in_specs=(spec, spec, lists, lists), out_specs=(spec,) * 5, check_vma=False
    )
```

```python
import jax
import jax.numpy as jnp
from jax import lax
from jax.experimental import pallas as pl
from jax.experimental.pallas import tpu as pltpu
from jax.sharding import PartitionSpec as P

F32 = jnp.float32
BF = jnp.bfloat16
R = 512
H = 256
T = 128
LIMIT = 28 << 20


def split2(x):
    hi = x.astype(BF)
    return hi, (x - hi.astype(F32)).astype(BF)


def split3(x):
    hi = x.astype(BF)
    rest = x - hi.astype(F32)
    mid = rest.astype(BF)
    return hi, mid, (rest - mid.astype(F32)).astype(BF)


def dot(a, b):
    return jnp.dot(a, b, preferred_element_type=F32)


def dot_tn(a, b):
    return lax.dot_general(a, b, (((0,), (0,)), ((), ())), preferred_element_type=F32)


def dot_nt(a, b):
    return lax.dot_general(a, b, (((1,), (1,)), ((), ())), preferred_element_type=F32)


def iota(shape, axis):
    return lax.broadcasted_iota(jnp.int32, shape, axis)


def pack_store(src, out):
    out[0:H, 0:H] = src[H:R, 0:H]
    rows, cols = iota((H, H), 0), iota((H, H), 1)
    first = src[0:H, 0:H]
    out[0:H, H:R] = jnp.where(rows >= cols, src[H:R, H:R], first)
    diag = jnp.sum(jnp.where(rows == cols, first, 0.0), axis=0, keepdims=True)
    out[H : H + 8, 0:H] = jnp.broadcast_to(diag, (8, H))
    out[H : H + 8, H:R] = jnp.zeros((8, H), F32)


def unpack_store(packed, out, base):
    low = packed[0:H, 0:H]
    mixed = packed[0:H, H:R]
    mixed_t = mixed.T
    rows, cols = iota((H, H), 0), iota((H, H), 1)
    diag = jnp.broadcast_to(packed[H : H + 1, 0:H], (H, H))
    first = jnp.where(rows < cols, mixed, mixed_t)
    out[base : base + H, 0:H] = jnp.where(rows == cols, diag, first)
    out[base : base + H, H:R] = low.T
    out[base + H : base + R, 0:H] = low
    out[base + H : base + R, H:R] = jnp.where(rows >= cols, mixed, mixed_t)


def pack_kernel(src, out):
    pack_store(src, out)


def pack(block):
    return pl.pallas_call(
        pack_kernel,
        out_shape=jax.ShapeDtypeStruct((H + 8, R), F32),
        compiler_params=pltpu.CompilerParams(vmem_limit_bytes=LIMIT),
        cost_estimate=pl.CostEstimate(flops=1 << 20, bytes_accessed=3 << 19, transcendentals=0),
        name="pack",
    )(block)


def index_column(order_row, start):
    row = order_row[0:1, start : start + T].astype(F32)
    return jnp.broadcast_to(row, (T, T)).T


def fill_rows_hot(order_row, out, base, width, side=None):
    for i in range(8):
        col = index_column(order_row, i * T)
        if side is not None:
            side[i * T : i * T + T, :] = jnp.where(col >= R, 1.0, 0.0)
        for c in range(width // T):
            lane = (iota((T, T), 1) + (base + c * T)).astype(F32)
            out[i * T : i * T + T, c * T : c * T + T] = jnp.where(col == lane, 1.0, 0.0).astype(BF)


def fill_cols_hot(order_row, out, base):
    order = jnp.broadcast_to(order_row[...], (R, 2 * R))
    out[...] = jnp.where(iota((R, 2 * R), 0) + base == order, 1.0, 0.0).astype(BF)


def halves(step):
    def run(i, carry):
        step(pl.ds(pl.multiple_of(i * R, R), R))
        return carry

    lax.fori_loop(0, 2, run, 0)


def spread_columns(block, cols_hot, parts):
    for i, piece in enumerate(split2(block)):
        parts[i] = dot(piece, cols_hot[...]).astype(BF)


def own_kernel(order_row, gen, block, main, tail, g_hi, g_lo, *rest):
    parent = rest[0] if len(rest) == 4 else None
    rows_hot, cols_hot, parts = rest[-3:]
    fill_rows_hot(order_row, rows_hot, 0, R)
    fill_cols_hot(order_row, cols_hot, 0)
    pieces = split3(gen[...])

    def pick(rows):
        g_hi[rows, :] = dot(rows_hot[rows, :], pieces[0]).astype(BF)
        g_lo[rows, :] = dot(rows_hot[rows, :], pieces[1]).astype(BF)

    halves(pick)
    if parent is not None:
        parent[...] = g_hi[R:].astype(F32) + g_lo[R:].astype(F32) + dot(rows_hot[R:], pieces[2])
    spread_columns(block[...], cols_hot, parts)

    def fill(rows):
        main[rows, :] = dot(rows_hot[rows, :], parts[0, :, :R]) + dot(rows_hot[rows, :], parts[1, :, :R])

    halves(fill)
    tail[...] = dot(rows_hot[R:, :], parts[0, :, R:]) + dot(rows_hot[R:, :], parts[1, :, R:])


def couple_kernel(order_row, gen, main_in, tail_in, g_hi, g_lo, *rest):
    with_parent = len(rest) == 8
    parent_in = rest[0] if with_parent else None
    main, tail = rest[1:3] if with_parent else rest[:2]
    parent = rest[3] if with_parent else None
    rows_hot, hi, lo, side = rest[-4:]
    fill_rows_hot(order_row, rows_hot, R, R, side)
    pieces = split3(gen[...])

    def pick(rows):
        hi[rows, :] = (g_hi[rows, :].astype(F32) + dot(rows_hot[rows, :], pieces[0])).astype(BF)
        lo[rows, :] = (g_lo[rows, :].astype(F32) + dot(rows_hot[rows, :], pieces[1])).astype(BF)

    halves(pick)
    if with_parent:
        high, mid, low = (dot(rows_hot[R:], piece) for piece in pieces)
        parent[...] = parent_in[...] + (high + mid + low)
    side_row = jnp.where(order_row[...] >= R, 1.0, 0.0)

    def fill(rows, cols, before, out, out_rows):
        coupling = dot_nt(hi[rows, :], hi[cols]) + dot_nt(hi[rows, :], lo[cols]) + dot_nt(lo[rows, :], hi[cols])
        out[out_rows, :] = before[out_rows, :] + jnp.where(side[rows, 0:1] != side_row[:, cols], coupling, 0.0)

    halves(lambda rows: fill(rows, slice(0, R), main_in, main, rows))
    fill(slice(R, 2 * R), slice(R, 2 * R), tail_in, tail, slice(0, R))


def place_own(order_row, gen, block, with_parent):
    vmem = pl.BlockSpec(memory_space=pltpu.VMEM)
    shapes = [((2 * R, R), F32), ((R, R), F32), ((2 * R, R), BF), ((2 * R, R), BF)] + [((R, R), F32)] * with_parent
    return pl.pallas_call(
        own_kernel,
        in_specs=[vmem] * 3,
        out_shape=tuple(jax.ShapeDtypeStruct(*s) for s in shapes),
        scratch_shapes=[pltpu.VMEM((2 * R, R), BF), pltpu.VMEM((R, 2 * R), BF), pltpu.VMEM((2, R, 2 * R), BF)],
        compiler_params=pltpu.CompilerParams(vmem_limit_bytes=LIMIT),
        cost_estimate=pl.CostEstimate(flops=5 << 30, bytes_accessed=6 << 20, transcendentals=0),
        name="place_own",
    )(order_row, gen, block)


def couple(order_row, gen, own):
    vmem = pl.BlockSpec(memory_space=pltpu.VMEM)
    shapes = [(2 * R, R), (R, R)] + [(R, R)] * (len(own) == 5)
    return pl.pallas_call(
        couple_kernel,
        in_specs=[vmem] * (2 + len(own)),
        out_shape=tuple(jax.ShapeDtypeStruct(s, F32) for s in shapes),
        scratch_shapes=[pltpu.VMEM((2 * R, R), BF)] * 3 + [pltpu.VMEM((2 * R, T), F32)],
        compiler_params=pltpu.CompilerParams(vmem_limit_bytes=LIMIT),
        cost_estimate=pl.CostEstimate(flops=5 << 30, bytes_accessed=6 << 20, transcendentals=0),
        name="couple",
    )(order_row, gen, *own)


def twice(x):
    return jnp.concatenate([x, x], 1)


def lane(block, at):
    return jnp.broadcast_to(block[:, at : at + 1], (8, T))


def factor_block(work):
    strips = 8
    rows = iota((8, 2 * T), 0)
    for base in range(0, T, 8 * strips):
        group = [work[base + 8 * t : base + 8 * t + 8, :] for t in range(strips)]
        outs = []
        following = None
        for s in range(strips):
            at = base + 8 * s
            strip = group[s]
            lines = [jnp.broadcast_to(strip[i : i + 1, :], (8, 2 * T)) for i in range(8)]
            own = following if following is not None else [lane(strip, at + k) for k in range(8)]
            small = {(i, k): jnp.broadcast_to(own[k][i : i + 1, :], (8, T)) for i in range(8) for k in range(i + 1)}
            below = {(t, k): lane(group[t], at + k) for t in range(s + 1, strips) for k in range(8)}
            following = [lane(group[s + 1], at + 8 + k) for k in range(8)] if s + 1 < strips else None
            out = None
            for j in range(8):
                inv = lax.rsqrt(small[j, j])
                line = lines[j] * twice(inv)
                out = line if out is None else jnp.where(rows == j, line, out)
                mult = {i: small[i, j] * inv for i in range(j + 1, 8)}
                for i in range(j + 1, 8):
                    for k in range(j + 1, i + 1):
                        small[i, k] = small[i, k] - mult[i] * mult[k]
                    lines[i] = lines[i] - twice(mult[i]) * line
                for t in range(s + 1, strips):
                    m = below[t, j] * inv
                    group[t] = group[t] - twice(m) * line
                    for k in range(j + 1, 8):
                        below[t, k] = below[t, k] - m * mult[k]
                    if t == s + 1:
                        for k in range(8):
                            following[k] = following[k] - m * jnp.broadcast_to(m[k : k + 1, :], (8, T))
            work[at : at + 8, :] = out
            outs.append(out)
        end = base + 8 * strips
        if end < T:
            h, m, l = split3(jnp.concatenate(outs, 0))
            left = jnp.concatenate([h, h, m, h, m, l], 0)
            right = jnp.concatenate([h, m, h, l, m, h], 0)
            work[end:, :] = work[end:, :] - dot_tn(left[:, end:T], right)


def product(a_hi, a_lo, b_hi, b_lo):
    return dot_nt(a_hi, b_hi) + dot_nt(a_hi, b_lo) + dot_nt(a_lo, b_hi)


def eliminate(mine, order_row, packed, main, tail, factor, area, kept, rows_hot, cols_hot, parts, full, hi, lo, work):
    unpack_store(packed, full, 0)
    fill_rows_hot(order_row, rows_hot, R, R)
    fill_cols_hot(order_row, cols_hot, R)
    kept_cols, all_cols = mine
    for i, piece in enumerate(split2(full[...])):
        parts[i, :, :R] = dot(piece, cols_hot[:, :R]).astype(BF)
        parts[i, :, all_cols] = dot(piece, cols_hot[:, all_cols]).astype(BF)

    def fill(rows):
        area[rows, :] = main[rows, :] + dot(rows_hot[rows, :], parts[0, :, :R]) + dot(rows_hot[rows, :], parts[1, :, :R])

    halves(fill)
    late = dot(rows_hot[R:, :], parts[0, :, all_cols]) + dot(rows_hot[R:, :], parts[1, :, all_cols])
    kept[:, kept_cols] = tail[:, kept_cols] + late
    eye = (iota((T, T), 0) == iota((T, T), 1)).astype(F32)
    upper = iota((T, T), 0) <= iota((T, T), 1)
    for k in range(4):
        o = k * T
        e = o + T
        diag = area[o:e, o:e]
        rest = area[e:, o:e]
        if k:
            diag = diag - product(hi[o:e, :o], lo[o:e, :o], hi[o:e, :o], lo[o:e, :o])
            rest = rest - product(hi[e:, :o], lo[e:, :o], hi[o:e, :o], lo[o:e, :o])
        slot = work.at[k]
        slot[:, :T] = diag
        slot[:, T:] = eye
        factor_block(slot)
        inv_hi, inv_lo = split2(slot[:, T:])
        rest_hi, rest_lo = split2(rest)
        solved = product(rest_hi, rest_lo, inv_hi, inv_lo)
        s_hi, s_lo = split2(solved)
        hi[e:, o:e] = s_hi
        lo[e:, o:e] = s_lo
        factor[o:e, o:e] = jnp.where(upper, slot[:, :T], 0.0).T
        if e < R:
            factor[e:, o:e] = solved[: R - e]
            factor[o:e, e:] = jnp.zeros((T, R - e), F32)
        area[R:, o:e] = solved[R - e :]


def low_kernel(place, order_row, packed, main, tail, f_out, p_out, s_out, k_out,
               factor, area, kept, rows_hot, cols_hot, parts, full, hi, lo, work):
    mine = (slice(0, R), slice(R, 2 * R))
    eliminate(mine, order_row, packed, main, tail, factor, area, kept, rows_hot, cols_hot, parts, full, hi, lo, work)
    s_out[...] = kept[...] - product(hi[R:], lo[R:], hi[R:], lo[R:])
    pack_store(s_out, k_out)
    at = pl.multiple_of(place[0] * H, H)
    f_out[...] = factor[:, pl.ds(at, H)]
    p_out[...] = area[pl.ds(R + at, H), :].T


def high_kernel(place, order_row, packed, main, tail, f_out, p_out, s_out,
                factor, area, kept, rows_hot, cols_hot, parts, full, hi, lo, work):
    at = pl.multiple_of(place[0] * T, T)
    columns = (pl.ds(at, T), pl.ds(pl.multiple_of(R + at, T), T))
    eliminate(columns, order_row, packed, main, tail, factor, area, kept, rows_hot, cols_hot, parts, full, hi, lo, work)
    mine = pl.ds(R + at, T)
    s_out[...] = kept[:, pl.ds(at, T)] - product(hi[R:], lo[R:], hi[mine, :], lo[mine, :])
    f_out[...] = factor[:, pl.ds(at, T)]
    p_out[...] = area[mine, :].T


def level(kernel, name, out_shapes, order_row, place, packed, main, tail):
    vmem = pl.BlockSpec(memory_space=pltpu.VMEM)
    smem = pl.BlockSpec(memory_space=pltpu.SMEM)
    return pl.pallas_call(
        kernel,
        in_specs=[smem, vmem, vmem, vmem, vmem],
        out_shape=tuple(jax.ShapeDtypeStruct(s, F32) for s in out_shapes),
        scratch_shapes=[
            pltpu.VMEM((R, R), F32),
            pltpu.VMEM((2 * R, R), F32),
            pltpu.VMEM((R, R), F32),
            pltpu.VMEM((2 * R, R), BF),
            pltpu.VMEM((R, 2 * R), BF),
            pltpu.VMEM((2, R, 2 * R), BF),
            pltpu.VMEM((R, R), F32),
            pltpu.VMEM((2 * R, R), BF),
            pltpu.VMEM((2 * R, R), BF),
            pltpu.VMEM((4, T, 2 * T), F32),
        ],
        compiler_params=pltpu.CompilerParams(vmem_limit_bytes=LIMIT),
        cost_estimate=pl.CostEstimate(flops=30 << 30, bytes_accessed=10 << 20, transcendentals=0),
        name=name,
    )(place, order_row, packed, main, tail)


def swap(value, axis):
    count = lax.axis_size(axis)
    return lax.ppermute(value, axis, [(i, (i + count // 2) % count) for i in range(count)])


def ordered(mine, theirs, parity):
    return jnp.where(parity == 0, jnp.concatenate((mine, theirs)), jnp.concatenate((theirs, mine)))


def body(skeleton, generator, skeleton_lists, upper_lists):
    tx_parity = lax.axis_index("tx") // (lax.axis_size("tx") // 2)
    ty_parity = lax.axis_index("ty") // (lax.axis_size("ty") // 2)
    block, gen = skeleton[0], generator[0]
    lists = jnp.concatenate((skeleton_lists[0, 0], upper_lists[0, 0]))
    got_lists = swap(lists, "tx")
    sent_gen, sent_block = lax.optimization_barrier((gen, block, got_lists))[:2]
    got_gen = swap(sent_gen, "tx")
    got_packed = swap(pack(sent_block), "tx")
    order_low = (ordered(lists[:R], got_lists[:R], tx_parity) ^ (tx_parity * R)).reshape(1, 2 * R)
    upper_own = ordered(lists[R:], got_lists[R:], tx_parity)
    upper_oth = swap(upper_own, "ty")
    order_high = (ordered(upper_own, upper_oth, ty_parity) ^ (ty_parity * R)).reshape(1, 2 * R)
    low_place = jnp.full((1,), tx_parity, jnp.int32)
    high_place = jnp.full((1,), 2 * ty_parity + tx_parity, jnp.int32)

    own = place_own(order_low, gen, block, True)
    got_gen = lax.optimization_barrier((got_gen, own[0], order_high))[0]
    main, tail, parent = couple(order_low, got_gen, own)
    oth_parent = swap(parent, "ty")
    factor_low, panel_low, schur, packed = level(
        low_kernel, "low", ((R, H), (R, H), (R, R), (H + 8, R)), order_low, low_place, got_packed, main, tail
    )
    oth_packed = swap(packed, "ty")
    own_high = place_own(order_high, parent, schur, False)
    oth_parent = lax.optimization_barrier((oth_parent, own_high[0]))[0]
    main_high, tail_high = couple(order_high, oth_parent, own_high)
    factor_high, panel_high, schur_high = level(
        high_kernel, "high", ((R, T), (R, T), (R, T)), order_high, high_place, oth_packed, main_high, tail_high
    )
    return factor_low[None], panel_low[None], factor_high[None], panel_high[None], schur_high[None]


def solution(mesh):
    spec = P(None, "tx", "ty")
    lists = P(None, "ty", "tx")
    return jax.shard_map(
        body, mesh=mesh, in_specs=(spec, spec, lists, lists), out_specs=(spec,) * 5, check_vma=False
    )
```
